512 devices in a mesh: lat: 16 (over z_lo, x, core), lon: 32 (over y, z_hi).
Axes of the slice: x: 4, y: 8, z: 8 (z_hi: 4, z_lo: 2; z = z_hi * 2 + z_lo), core: 2. Of those that a mesh axis runs over, the one named last changes fastest.
Arguments:
- fine_query: bfloat16 [384, 1024, 512], P('lat', 'lon'), may hold values from -6 to 6
- fine_keyval: bfloat16 [384, 1024, 1024], P('lat', 'lon'), may hold values from -6 to 6
- coarse_query: bfloat16 [96, 256, 512], P('lat', 'lon'), may hold values from -6 to 6
- coarse_keyval: bfloat16 [96, 256, 1024], P('lat', 'lon'), may hold values from -6 to 6
- out_weight: bfloat16 [512, 512], replicated, may hold values from -0.25 to 0.25
Outputs:
- output: bfloat16 [384, 1024, 512], P('lat', 'lon')
The draws below stay inside these ranges and needn't reach their ends.
All inputs are finite; a program needn't handle non-finite values.
Results may differ from the reference program's by a relative error of at most 0.0061.
Values may be sent and summed in bfloat16 or wider, within the bound.
A program may use at most 64 MiB of HBM per device.

```python
import math
import jax
import jax.numpy as jnp
from jax import lax

HEADS = 8
D = 512
RADIUS = 6
FH = 24
FW = 32
CH = 6
CW = 8
NLAT = 384
NLON = 1024
CLAT = 96
CLON = 256
N_LAT = 16
N_LON = 32


def rough_field(key, shape, spread):
    values = jax.random.normal(key, shape) * spread
    return jnp.clip(values.astype(jnp.float32), -6.0, 6.0)


def draw_fine_query(key, part):
    values = rough_field(jax.random.fold_in(key, 1), (NLAT, NLON, D), 1.4)
    return values.astype(jnp.bfloat16)


def draw_fine_keyval(key, part):
    key_portion = rough_field(jax.random.fold_in(key, 2), (NLAT, NLON, D), 1.4)
    value_portion = rough_field(jax.random.fold_in(key, 3), (NLAT, NLON, D), 1.0)
    return jnp.concatenate([key_portion, value_portion], axis=-1).astype(jnp.bfloat16)


def draw_coarse_query(key, part):
    values = rough_field(jax.random.fold_in(key, 4), (CLAT, CLON, D), 1.4)
    return values.astype(jnp.bfloat16)


def draw_coarse_keyval(key, part):
    key_portion = rough_field(jax.random.fold_in(key, 5), (CLAT, CLON, D), 1.4)
    value_portion = rough_field(jax.random.fold_in(key, 6), (CLAT, CLON, D), 1.0)
    return jnp.concatenate([key_portion, value_portion], axis=-1).astype(jnp.bfloat16)


def centred(own_key, shape, deviation, reach, held_as=jnp.bfloat16):
    drawn = jax.random.normal(own_key, shape, jnp.float32) * deviation
    return jnp.minimum(jnp.maximum(drawn, -reach), reach).astype(held_as)


def setup_inputs(seed: int = 0) -> dict:
    splits = jax.random.split(jax.random.key(seed), 6)
    return {
        "fine_query": draw_fine_query(jax.random.fold_in(splits[5], 71), 0),
        "fine_keyval": draw_fine_keyval(jax.random.fold_in(splits[5], 71), 0),
        "coarse_query": draw_coarse_query(jax.random.fold_in(splits[5], 71), 0),
        "coarse_keyval": draw_coarse_keyval(jax.random.fold_in(splits[5], 71), 0),
        "out_weight": centred(splits[4], (D, D), D ** -0.5, 0.25),
    }


NEGATIVE = -1e+30

def window_allowed(tile_rows, tile_cols, radius, rows_valid):
    ext_rows = tile_rows + 2 * radius
    ext_cols = tile_cols + 2 * radius
    query_pos = jnp.arange(tile_rows * tile_cols, dtype=jnp.int32)
    key_pos = jnp.arange(ext_rows * ext_cols, dtype=jnp.int32)
    lat_gap = (key_pos // ext_cols)[None, :] - radius - (query_pos // tile_cols)[:, None]
    lon_gap = (key_pos % ext_cols)[None, :] - radius - (query_pos % tile_cols)[:, None]
    key_valid = jnp.repeat(rows_valid, ext_cols)
    return (jnp.abs(lat_gap) <= radius) & (jnp.abs(lon_gap) <= radius) & key_valid[None, :]

def rows_inside(tile_index, tile_rows, radius, total_rows):
    global_rows = tile_index * tile_rows - radius + jnp.arange(tile_rows + 2 * radius, dtype=jnp.int32)
    return (global_rows >= 0) & (global_rows < total_rows)

def attend(queries, keyval, allowed, head_count):
    length, channels = queries.shape
    head_dim = channels // head_count
    scaling_factor = 1.0 / math.sqrt(head_dim)
    query_portion = queries.astype(jnp.float32).reshape(length, head_count, head_dim)
    key_portion = keyval[:, :channels].astype(jnp.float32).reshape(-1, head_count, head_dim)
    value_portion = keyval[:, channels:].astype(jnp.float32).reshape(-1, head_count, head_dim)
    logit_scores = jnp.einsum('qkf,okf->kqo', query_portion, key_portion, precision=lax.Precision.HIGHEST) * scaling_factor
    if allowed is not None:
        logit_scores = jnp.where(allowed[None, :, :], logit_scores, NEGATIVE)
    logit_scores = logit_scores - lax.optimization_barrier(jnp.max(logit_scores, axis=-1, keepdims=True))
    raised = jnp.exp(logit_scores)
    softmax_weights = (raised / lax.optimization_barrier(jnp.sum(raised, axis=-1, keepdims=True))).astype(jnp.bfloat16)
    blended_output = jnp.einsum('ekp,peu->keu', softmax_weights.astype(jnp.float32), value_portion, precision=lax.Precision.HIGHEST)
    return blended_output.reshape(length, channels)

def upsample_table(fine_size):
    fine_index = jnp.arange(fine_size, dtype=jnp.int32)
    coarse_index = fine_index // 4
    offset = ((fine_index % 4).astype(jnp.float32) - 1.5) / 4.0
    columns = jnp.arange(fine_size // 4 + 2, dtype=jnp.int32)
    before = jnp.where(offset < 0, -offset, 0.0)
    after = jnp.where(offset > 0, offset, 0.0)
    centre = 1.0 - jnp.abs(offset)
    table = jnp.where(columns[None, :] == coarse_index[:, None], before[:, None], 0.0)
    table = table + jnp.where(columns[None, :] == coarse_index[:, None] + 1, centre[:, None], 0.0)
    table = table + jnp.where(columns[None, :] == coarse_index[:, None] + 2, after[:, None], 0.0)
    return table.astype(jnp.float32)

def upsample(coarse, lat_table, lon_table):
    halfway = jnp.einsum('ia,abc->ibc', lat_table, coarse.astype(jnp.float32), precision=lax.Precision.HIGHEST)
    return jnp.einsum('jb,ibc->ijc', lon_table, halfway, precision=lax.Precision.HIGHEST)

def reference(fine_query, fine_keyval, coarse_query, coarse_keyval, out_weight):
    tiles = N_LAT * N_LON
    tile_ids = jnp.arange(tiles, dtype=jnp.int32)
    zero = jnp.zeros((), jnp.int32)

    def coarse_tile(tile):
        tile_lat = tile // N_LON
        tile_lon = tile % N_LON
        lat_rows = tile_lat * CH - RADIUS + jnp.arange(CH + 2 * RADIUS, dtype=jnp.int32)
        lon_cols = (tile_lon * CW - RADIUS + jnp.arange(CW + 2 * RADIUS, dtype=jnp.int32)) % CLON
        extended = jnp.take(jnp.take(coarse_keyval, lon_cols, axis=1), jnp.clip(lat_rows, 0, CLAT - 1), axis=0)
        queries = lax.dynamic_slice(coarse_query, ((tile_lat * CH).astype(jnp.int32), (tile_lon * CW).astype(jnp.int32), zero), (CH, CW, D))
        allowed = window_allowed(CH, CW, RADIUS, rows_inside(tile_lat, CH, RADIUS, CLAT))
        return attend(queries.reshape(-1, D), extended.reshape(-1, 2 * D), allowed, HEADS).astype(jnp.bfloat16)
    coarse_att = lax.map(coarse_tile, tile_ids)
    coarse_att = coarse_att.reshape(N_LAT, N_LON, CH, CW, D).transpose(0, 2, 1, 3, 4).reshape(CLAT, CLON, D)
    lat_table = upsample_table(FH)
    lon_table = upsample_table(FW)

    def fine_tile(tile):
        tile_lat = tile // N_LON
        tile_lon = tile % N_LON
        lat_rows = tile_lat * FH - RADIUS + jnp.arange(FH + 2 * RADIUS, dtype=jnp.int32)
        lon_cols = (tile_lon * FW - RADIUS + jnp.arange(FW + 2 * RADIUS, dtype=jnp.int32)) % NLON
        extended = jnp.take(jnp.take(fine_keyval, lon_cols, axis=1), jnp.clip(lat_rows, 0, NLAT - 1), axis=0)
        queries = lax.dynamic_slice(fine_query, ((tile_lat * FH).astype(jnp.int32), (tile_lon * FW).astype(jnp.int32), zero), (FH, FW, D)).reshape(-1, D)
        allowed = window_allowed(FH, FW, RADIUS, rows_inside(tile_lat, FH, RADIUS, NLAT))
        fine_att = attend(queries, extended.reshape(-1, 2 * D), allowed, HEADS).astype(jnp.bfloat16)
        cycle_rows = jnp.clip(tile_lat * CH - 1 + jnp.arange(CH + 2, dtype=jnp.int32), 0, CLAT - 1)
        cycle_cols = (tile_lon * CW - 1 + jnp.arange(CW + 2, dtype=jnp.int32)) % CLON
        cycle_keyval = jnp.take(jnp.take(coarse_keyval, cycle_cols, axis=1), cycle_rows, axis=0)
        cycle_att = jnp.take(jnp.take(coarse_att, cycle_cols, axis=1), cycle_rows, axis=0)
        up_keyval = upsample(cycle_keyval, lat_table, lon_table).astype(jnp.bfloat16).reshape(-1, 2 * D)
        up_att = upsample(cycle_att, lat_table, lon_table).reshape(-1, D)
        cross = attend(queries, up_keyval, None, HEADS)
        joined = (fine_att.astype(jnp.float32) + cross + up_att).astype(jnp.bfloat16)
        return jnp.dot(joined, out_weight, preferred_element_type=jnp.float32).astype(jnp.bfloat16)
    output = lax.map(fine_tile, tile_ids)
    return output.reshape(N_LAT, N_LON, FH, FW, D).transpose(0, 2, 1, 3, 4).reshape(NLAT, NLON, D)
```

```python
import functools

import jax
import jax.numpy as jnp
from jax import lax
from jax.experimental import pallas as pl
from jax.experimental.pallas import tpu as pltpu
from jax.sharding import PartitionSpec as P

RADIUS = 6
FH, FW, CH, CW, D = 24, 32, 6, 8, 512
PAD = 8
ROWS = 8
COLS = 16
BLOCKS = FH // ROWS
KROWS = ROWS + 2 * RADIUS
KEYS = KROWS * 2 * COLS
CKEYS = 3 * CH * 3 * CW
CYCLE = (CH + 2) * 3 * CW
BIG = 2.0**100
LOG2E = 1.4426950408889634
MESH = pl.DeviceIdType.MESH
F32, BF16 = jnp.float32, jnp.bfloat16


def iota(shape, dim):
    return lax.broadcasted_iota(jnp.int32, shape, dim)


def dot_nt(a, b):
    return lax.dot_general(a, b, (((1,), (1,)), ((), ())), preferred_element_type=F32)


def dot(a, b):
    return jnp.dot(a, b, preferred_element_type=F32)


def head_masks(value):
    first = iota((1, 128), 1) < 64
    low = jnp.where(first, value, 0.0).astype(BF16)
    high = jnp.where(first, 0.0, value).astype(BF16)
    return first, low, high


def query_marks(rows, cols):
    shape = (rows * cols, 128)
    pos, lane = iota(shape, 0), iota(shape, 1)
    hit = (lane == pos // cols) & (lane < 16)
    hit = hit | (lane == pos % cols + 16) | (lane == 32)
    return jnp.where(hit, 1.0, 0.0).astype(BF16)


def key_marks(rows, cols, col_shift, first_row, row_count):
    shape = (rows * cols, 128)
    pos, lane = iota(shape, 0), iota(shape, 1)
    row, col = pos // cols, pos % cols
    row_out = (lane < 16) & ((row < lane) | (row > lane + 2 * RADIUS))
    gap = col - col_shift - (lane - 16)
    col_out = (lane >= 16) & (lane < 32) & ((gap > RADIUS) | (gap < -RADIUS))
    place = row + first_row
    bad = (lane == 32) & ((place < 0) | (place >= row_count))
    return jnp.where(row_out | col_out | bad, -BIG, 0.0).astype(BF16)


def attend(lhs, keys, values, first, base2):
    scores = dot_nt(lhs, keys)
    scores = scores - jnp.max(scores, axis=1, keepdims=True)
    raised = (jnp.exp2(scores) if base2 else jnp.exp(scores)).astype(BF16)
    both = dot(raised, values)
    both = both[:, :128] / both[:, 128:]
    half = both.shape[0] // 2
    return jnp.where(first, both[:half], both[half:])


def spread_table(lat, lats):
    shape = (FH * FW, CYCLE)
    pos, key = iota(shape, 0), iota(shape, 1)
    i, j, a, b = pos // FW, pos % FW, key // (3 * CW), key % (3 * CW) - (CW - 1)

    def weights(fine, coarse, lowest, highest):
        offset = ((fine % 4).astype(F32) - 1.5) / 4.0
        base = fine // 4
        total = jnp.where(
            coarse == jnp.minimum(jnp.maximum(base, lowest), highest),
            jnp.maximum(-offset, 0.0),
            0.0,
        )
        total = total + jnp.where(
            coarse == jnp.minimum(jnp.maximum(base + 1, lowest), highest),
            1.0 - jnp.abs(offset),
            0.0,
        )
        return total + jnp.where(
            coarse == jnp.minimum(jnp.maximum(base + 2, lowest), highest),
            jnp.maximum(offset, 0.0),
            0.0,
        )

    lowest = jnp.where(lat == 0, 1, 0)
    highest = jnp.where(lat == lats - 1, CH, CH + 1)
    return (weights(i, a, lowest, highest) * weights(j, b, 0, CW + 1)).astype(BF16)


def kernel(
    lats, lons, fq_hbm, fkv_hbm, cq_hbm, ckv_hbm, w_hbm, out_hbm,
    fq, ext, cq, cext, w, cflat, attx, table, upkv, fmarks, acc, outv,
    local, send, recv, osem,
):
    lat, lon = lax.axis_index("lat"), lax.axis_index("lon")
    up, down = lax.rem(lat + lats - 1, lats), lax.rem(lat + 1, lats)
    left, right = lax.rem(lon + lons - 1, lons), lax.rem(lon + 1, lons)

    loads = [
        pltpu.make_async_copy(ckv_hbm, cext.at[CH : 2 * CH, CW : 2 * CW], local.at[0]),
        pltpu.make_async_copy(cq_hbm, cq, local.at[1]),
        pltpu.make_async_copy(fq_hbm, fq, local.at[2]),
        pltpu.make_async_copy(
            fkv_hbm, ext.at[RADIUS : RADIUS + FH, PAD : PAD + FW], local.at[3]
        ),
        pltpu.make_async_copy(w_hbm, w, local.at[4]),
    ]
    for load in loads:
        load.start()

    barrier = pltpu.get_barrier_semaphore()
    for other in (
        (up, lon), (down, lon), (lat, left), (lat, right),
        (up, left), (up, right), (down, left), (down, right),
    ):
        pl.semaphore_signal(barrier, inc=1, device_id=other, device_id_type=MESH)
    pl.semaphore_wait(barrier, 8)

    def remote(number, source, target, device):
        return pltpu.make_async_remote_copy(
            src_ref=source, dst_ref=target, send_sem=send.at[number],
            recv_sem=recv.at[number], device_id=device, device_id_type=MESH,
        )

    mid = slice(CH, 2 * CH)
    coarse_lon = [
        remote(0, ckv_hbm, cext.at[mid, 0:CW], (lat, right)),
        remote(1, ckv_hbm, cext.at[mid, 2 * CW : 3 * CW], (lat, left)),
    ]
    coarse_lat = [
        remote(2, ckv_hbm, cext.at[0:CH, CW : 2 * CW], (down, lon)),
        remote(3, ckv_hbm, cext.at[2 * CH : 3 * CH, CW : 2 * CW], (up, lon)),
    ]
    coarse_corner = [
        remote(4 + 2 * n + m, cext.at[mid, side], cext.at[rows, side], device)
        for n, side in enumerate((slice(0, CW), slice(2 * CW, 3 * CW)))
        for m, (rows, device) in enumerate(
            ((slice(0, CH), (down, lon)), (slice(2 * CH, 3 * CH), (up, lon)))
        )
    ]
    own_rows = slice(RADIUS, RADIUS + FH)
    own_cols = slice(PAD, PAD + FW)
    last_cols = slice(PAD + FW, 2 * PAD + FW)
    top, bottom = slice(0, RADIUS), slice(RADIUS + FH, 2 * RADIUS + FH)
    fine_lon = [
        remote(8, fkv_hbm.at[:, FW - PAD : FW], ext.at[own_rows, 0:PAD], (lat, right)),
        remote(9, fkv_hbm.at[:, 0:PAD], ext.at[own_rows, last_cols], (lat, left)),
    ]
    fine_lat = [
        remote(10, fkv_hbm.at[FH - RADIUS : FH], ext.at[top, own_cols], (down, lon)),
        remote(11, fkv_hbm.at[0:RADIUS], ext.at[bottom, own_cols], (up, lon)),
    ]
    fine_corner = [
        remote(12 + 2 * n + m, ext.at[source, side], ext.at[rows, side], device)
        for n, side in enumerate((slice(0, PAD), last_cols))
        for m, (source, rows, device) in enumerate(
            (
                (slice(FH, FH + RADIUS), top, (down, lon)),
                (slice(RADIUS, 2 * RADIUS), bottom, (up, lon)),
            )
        )
    ]
    whole, first_row, last_row = slice(1, CH + 1), slice(1, 2), slice(CH, CH + 1)
    above, below = slice(0, 1), slice(CH + 1, CH + 2)
    centre, west, east = slice(CW, 2 * CW), slice(0, CW), slice(2 * CW, 3 * CW)
    att_moves = [
        remote(16 + n, attx.at[rows, centre], attx.at[to_rows, to_cols], device)
        for n, (rows, to_rows, to_cols, device) in enumerate(
            (
                (whole, whole, west, (lat, right)),
                (whole, whole, east, (lat, left)),
                (last_row, above, centre, (down, lon)),
                (first_row, below, centre, (up, lon)),
                (last_row, above, west, (down, right)),
                (last_row, above, east, (down, left)),
                (first_row, below, west, (up, right)),
                (first_row, below, east, (up, left)),
            )
        )
    ]

    for copy in coarse_lon + coarse_lat + fine_lon + fine_lat:
        copy.start()

    table[...] = spread_table(lat, lats)
    for block in range(BLOCKS):
        fmarks[block] = key_marks(
            KROWS, 2 * COLS, PAD, lat * FH + block * ROWS - RADIUS, lats * FH
        )
    fine_marks = query_marks(ROWS, COLS)
    cq_marks = query_marks(CH, CW)
    ckey_marks = key_marks(3 * CH, 3 * CW, CW, (lat - 1) * CH, lats * CH)

    for copy in coarse_lon:
        copy.wait_recv()
    for copy in coarse_corner:
        copy.start()
    for copy in coarse_lat + coarse_corner:
        copy.wait_recv()
    loads[0].wait()
    loads[1].wait()

    cflat[...] = cext[...].astype(F32).reshape(CKEYS, 2 * D).astype(BF16)
    first, low, high = head_masks(0.125)
    cones = jnp.ones((CKEYS, 128), BF16)
    for pair in range(4):
        lanes = slice(pair * 128, pair * 128 + 128)
        vlanes = slice(D + pair * 128, D + pair * 128 + 128)
        query = cq[:, :, lanes].astype(F32).reshape(CH * CW, 128).astype(BF16)
        lhs = jnp.concatenate(
            [
                jnp.concatenate([query * low, cq_marks], 1),
                jnp.concatenate([query * high, cq_marks], 1),
            ],
            0,
        )
        keys = jnp.concatenate([cflat[:, lanes], ckey_marks], 1)
        values = jnp.concatenate([cflat[:, vlanes], cones], 1)
        att = attend(lhs, keys, values, first, False)
        attx[1 : CH + 1, CW : 2 * CW, lanes] = att.reshape(CH, CW, 128).astype(BF16)
    for copy in att_moves:
        copy.start()

    start = (CH - 1) * 3 * CW
    for part in range(4):
        lanes = slice(part * 256, part * 256 + 256)
        upkv[:, lanes] = dot(table[...], cflat[start : start + CYCLE, lanes]).astype(BF16)

    loads[2].wait()
    ones = jnp.ones((FH * FW, 128), BF16)
    _, low1, high1 = head_masks(1.0)
    for pair in range(4):
        lanes = slice(pair * 128, pair * 128 + 128)
        vlanes = slice(D + pair * 128, D + pair * 128 + 128)
        query = fq[:, :, lanes].reshape(FH * FW, 128).astype(F32) * (0.125 * LOG2E)
        coarse_part = query.astype(BF16)
        rest = (query - coarse_part.astype(F32)).astype(BF16)
        keys = jnp.concatenate([upkv[:, lanes], upkv[:, lanes]], 1)
        values = jnp.concatenate([upkv[:, vlanes], ones], 1)
        outs = []
        for mask in (low1, high1):
            scores = dot_nt(jnp.concatenate([coarse_part * mask, rest * mask], 1), keys)
            scores = scores - jnp.max(scores, axis=1, keepdims=True)
            both = dot(jnp.exp2(scores).astype(BF16), values)
            outs.append(both[:, :128] / both[:, 128:])
        cross = jnp.where(first, outs[0], outs[1])
        acc[:, :, lanes] = cross.reshape(FH, FW, 128)

    for copy in fine_lon:
        copy.wait_recv()
    for copy in fine_corner:
        copy.start()
    loads[3].wait()
    loads[4].wait()

    kones = jnp.ones((KEYS, 128), BF16)

    def fine_block(block, half):
        r0 = block * ROWS
        c0 = pl.multiple_of(half * COLS, COLS)
        rows, cols = pl.ds(r0, ROWS), pl.ds(c0, COLS)
        krows, kcols = pl.ds(r0, KROWS), pl.ds(c0, 2 * COLS)
        marks = fmarks[block]
        for pair in range(4):
            lanes = slice(pair * 128, pair * 128 + 128)
            vlanes = slice(D + pair * 128, D + pair * 128 + 128)
            query = fq[rows, cols, lanes].reshape(ROWS * COLS, 128)
            lhs = jnp.concatenate(
                [
                    jnp.concatenate([query * low, fine_marks], 1),
                    jnp.concatenate([query * high, fine_marks], 1),
                ],
                0,
            )
            keys = jnp.concatenate([ext[krows, kcols, lanes].reshape(KEYS, 128), marks], 1)
            values = jnp.concatenate([ext[krows, kcols, vlanes].reshape(KEYS, 128), kones], 1)
            att = attend(lhs, keys, values, first, False).astype(BF16).astype(F32)
            acc[rows, cols, lanes] += att.reshape(ROWS, COLS, 128)

    def middle(half, carry):
        fine_block(1, half)
        return carry

    def outer(step, carry):
        fine_block(2 * (step // 2), step % 2)
        return carry

    lax.fori_loop(0, 2, middle, 0)
    for copy in fine_lat + fine_corner:
        copy.wait_recv()
    lax.fori_loop(0, 4, outer, 0)

    for copy in att_moves:
        copy.wait_recv()
    aflat = attx[...].astype(F32).reshape(CYCLE, D).astype(BF16)
    up_att = dot(table[...], aflat)
    joined = (acc[...].reshape(FH * FW, D) + up_att).astype(BF16)
    outv[...] = dot(joined, w[...]).astype(BF16).reshape(FH, FW, D)
    store = pltpu.make_async_copy(outv, out_hbm, osem)
    store.start()
    for copy in coarse_lon + coarse_lat + coarse_corner + fine_lon + fine_lat:
        copy.wait_send()
    for copy in fine_corner + att_moves:
        copy.wait_send()
    store.wait()


def shards(fine_query, fine_keyval, coarse_query, coarse_keyval, out_weight):
    lats, lons = lax.axis_size("lat"), lax.axis_size("lon")
    anywhere = pl.BlockSpec(memory_space=pl.ANY)
    dma = pltpu.SemaphoreType.DMA
    return pl.pallas_call(
        functools.partial(kernel, lats, lons),
        out_shape=jax.ShapeDtypeStruct(fine_query.shape, BF16),
        in_specs=[anywhere] * 5,
        out_specs=anywhere,
        scratch_shapes=[
            pltpu.VMEM((FH, FW, D), BF16),
            pltpu.VMEM((FH + 2 * RADIUS, FW + 2 * PAD, 2 * D), BF16),
            pltpu.VMEM((CH, CW, D), BF16),
            pltpu.VMEM((3 * CH, 3 * CW, 2 * D), BF16),
            pltpu.VMEM((D, D), BF16),
            pltpu.VMEM((CKEYS, 2 * D), BF16),
            pltpu.VMEM((CH + 2, 3 * CW, D), BF16),
            pltpu.VMEM((FH * FW, CYCLE), BF16),
            pltpu.VMEM((FH * FW, 2 * D), BF16),
            pltpu.VMEM((BLOCKS, KEYS, 128), BF16),
            pltpu.VMEM((FH, FW, D), F32),
            pltpu.VMEM((FH, FW, D), BF16),
            dma((5,)),
            dma((24,)),
            dma((24,)),
            dma,
        ],
        compiler_params=pltpu.CompilerParams(
            collective_id=0, has_side_effects=True, vmem_limit_bytes=56 << 20
        ),
        name="neighbourhood",
    )(fine_query, fine_keyval, coarse_query, coarse_keyval, out_weight)


def solution(mesh):
    tile = P("lat", "lon", None)
    return jax.shard_map(
        shards, mesh=mesh, in_specs=(tile, tile, tile, tile, P()), out_specs=tile,
        check_vma=False,
    )
```

```python
import functools

import jax
import jax.numpy as jnp
from jax import lax
from jax.experimental import pallas as pl
from jax.experimental.pallas import tpu as pltpu
from jax.sharding import PartitionSpec as P

RADIUS = 6
FH, FW, CH, CW, D = 24, 32, 6, 8, 512
CELLS = FH * FW
EDGE = FH * RADIUS
CORNER = 40
PAD = 56
SIDE = EDGE + 2 * PAD
CAP = RADIUS * FW
CKEYS = 3 * CH * 3 * CW
CYCLE = (CH + 2) * 3 * CW
ATTS = CH * CW + 64
BIG = 2.0**100
LOG2E = 1.4426950408889634
MESH = pl.DeviceIdType.MESH
F32, BF16 = jnp.float32, jnp.bfloat16


def iota(shape, dim):
    return lax.broadcasted_iota(jnp.int32, shape, dim)


def dot_nt(a, b):
    return lax.dot_general(a, b, (((1,), (1,)), ((), ())), preferred_element_type=F32)


def dot(a, b):
    return jnp.dot(a, b, preferred_element_type=F32)


def flat(block):
    return block.astype(F32).reshape(-1, block.shape[-1]).astype(BF16)


def query_marks(row, col, count):
    lane = iota((count, 128), 1)
    hit = (lane == row) | (lane == col + 32) | (lane == 64)
    return jnp.where(hit, 1.0, 0.0).astype(BF16)


def key_marks(row, col, count, first_row, row_count):
    lane = iota((count, 128), 1)
    row_out = (lane < 24) & (jnp.abs(row - lane) > RADIUS)
    col_out = (lane >= 32) & (lane < 64) & (jnp.abs(col - lane + 32) > RADIUS)
    place = row + first_row
    bad = (lane == 64) & ((place < 0) | (place >= row_count))
    return jnp.where(row_out | col_out | bad, -BIG, 0.0).astype(BF16)


def attend(query, marks, keys, values, base2=False, stack=False):
    parts = []
    if marks is not None:
        query = [jnp.concatenate([head, marks], 1) for head in query]
    for head in [jnp.concatenate(query, 0)] if stack else query:
        scores = dot_nt(head, keys)
        top = jnp.max(scores, axis=1, keepdims=True)
        raised = jnp.exp2(scores - top) if base2 else jnp.exp(scores - top)
        both = dot(raised.astype(BF16), values)
        parts.append((both[:, :128], both[:, 128:], top))
    first = iota((1, 128), 1) < 64
    if stack:
        half = query[0].shape[0]
        parts = [[x[:half] for x in parts[0]], [x[half:] for x in parts[0]]]
    return [jnp.where(first, low, high) for low, high in zip(*parts)]


def hat(x, place):
    return jnp.maximum(1.0 - jnp.abs(x - place), 0.0)


def spread(a, b, lat, lats):
    pos = iota((CELLS, 1), 0)
    x = ((pos // FW).astype(F32) - 1.5) / 4.0
    x = jnp.maximum(x, jnp.where(lat == 0, 0.0, -1.0))
    x = jnp.minimum(x, jnp.where(lat == lats - 1, CH - 1.0, CH + 0.0))
    y = ((pos % FW).astype(F32) - 1.5) / 4.0
    return (hat(x, a.astype(F32)) * hat(y, b.astype(F32))).astype(BF16)


def att_places():
    n = iota((1, ATTS), 1)
    a, b = n // CW, n % CW
    group, k = n // 8, n % 8
    far = -100
    a = jnp.where((group == 6) | (group == 7), jnp.where(k < CH, k, far), a)
    b = jnp.where(group == 6, -1, jnp.where(group == 7, CW, b))
    a = jnp.where(group == 8, -1, jnp.where(group == 9, CH, a))
    a = jnp.where((group == 10) | (group == 11), -1, a)
    a = jnp.where((group == 12) | (group == 13), CH, a)
    b = jnp.where((group == 10) | (group == 12), jnp.where(k == CW - 1, -1, far), b)
    b = jnp.where((group == 11) | (group == 13), jnp.where(k == 0, CW, far), b)
    return a, b


def kernel(
    lats, lons, fq_hbm, fkv_hbm, cq_hbm, ckv_hbm, w_hbm, out_hbm,
    fq, own, cq, cext, w, packed, sides, caps, cflat, atts, edges, table, table2, upkv,
    own_marks, side_marks, cap_marks, total, weight, largest, acc, outv,
    local, send, recv, osem,
):
    lat, lon = lax.axis_index("lat"), lax.axis_index("lon")
    up, down = lax.rem(lat + lats - 1, lats), lax.rem(lat + 1, lats)
    left, right = lax.rem(lon + lons - 1, lons), lax.rem(lon + 1, lons)

    loads = [
        pltpu.make_async_copy(fkv_hbm, own, local.at[0]),
        pltpu.make_async_copy(ckv_hbm, cext.at[CH : 2 * CH, CW : 2 * CW], local.at[1]),
        pltpu.make_async_copy(fq_hbm, fq, local.at[2]),
        pltpu.make_async_copy(cq_hbm, cq, local.at[3]),
        pltpu.make_async_copy(w_hbm, w, local.at[4]),
    ]
    for load in loads:
        load.start()

    barrier = pltpu.get_barrier_semaphore()
    for other in (
        (up, lon), (down, lon), (lat, left), (lat, right),
        (up, left), (up, right), (down, left), (down, right),
    ):
        pl.semaphore_signal(barrier, inc=1, device_id=other, device_id_type=MESH)
    middle = lats // 2
    not_top, not_last = lat != 0, lat != lats - 1
    relay = (lat == 0) | (lat == lats - 1)
    linked = relay | (lat == middle - 1) | (lat == middle)
    across = lax.rem(lat + middle, lats)
    beside = jnp.where(lat < middle, middle - 1 - lat, lats + middle - 1 - lat)

    @pl.when(linked)
    def _():
        for other in (across, beside):
            pl.semaphore_signal(barrier, inc=1, device_id=(other, lon), device_id_type=MESH)

    def remote(number, source, target, device):
        return pltpu.make_async_remote_copy(
            src_ref=source, dst_ref=target, send_sem=send.at[number],
            recv_sem=recv.at[number], device_id=device, device_id_type=MESH,
        )

    mid = slice(CH, 2 * CH)
    west, centre, east = slice(0, CW), slice(CW, 2 * CW), slice(2 * CW, 3 * CW)
    coarse_lon = [
        remote(0, ckv_hbm, cext.at[mid, west], (lat, right)),
        remote(1, ckv_hbm, cext.at[mid, east], (lat, left)),
    ]
    coarse_lat = [
        remote(2, ckv_hbm, cext.at[0:CH, centre], (down, lon)),
        remote(3, ckv_hbm, cext.at[2 * CH : 3 * CH, centre], (up, lon)),
    ]
    coarse_corner = [
        remote(4 + 2 * n + m, cext.at[mid, side], cext.at[rows, side], device)
        for n, side in enumerate((west, east))
        for m, (rows, device) in enumerate(
            ((slice(0, CH), (down, lon)), (slice(2 * CH, 3 * CH), (up, lon)))
        )
    ]
    strip = slice(PAD, PAD + EDGE)
    fine_lon = [
        remote(8, packed.at[1], sides.at[0, strip], (lat, right)),
        remote(9, packed.at[0], sides.at[1, strip], (lat, left)),
    ]
    via_top, via_last = lat == middle - 1, lat == middle

    def cap_move(number, arrival, source, slot, device):
        return pltpu.make_async_remote_copy(
            src_ref=source, dst_ref=caps.at[slot], send_sem=send.at[number],
            recv_sem=recv.at[arrival], device_id=(device, lon), device_id_type=MESH,
        )

    cap_down = cap_move(
        10, jnp.where(via_top, 24, 10), fkv_hbm.at[FH - RADIUS : FH],
        jnp.where(via_top, 2, 0), jnp.where(via_top, 0, down),
    )
    cap_up = cap_move(
        11, jnp.where(via_last, 24, 11), fkv_hbm.at[0:RADIUS],
        jnp.where(via_last, 2, 1), jnp.where(via_last, lats - 1, up),
    )
    cap_on = cap_move(
        24, jnp.where(lat == 0, 10, 11), caps.at[2],
        jnp.where(lat == 0, 0, 1), jnp.where(lat == 0, middle, middle - 1),
    )
    relayed = remote(24, fkv_hbm.at[0:RADIUS], caps.at[2], (lat, right))
    cap_from = [
        remote(10, fkv_hbm.at[0:RADIUS], caps.at[0], (lat, right)),
        remote(11, fkv_hbm.at[0:RADIUS], caps.at[1], (lat, right)),
    ]

    def when_down(action, *copies):
        @pl.when(not_last)
        def _():
            for copy in copies:
                getattr(copy, action)()

    def when_up(action, *copies):
        @pl.when(not_top)
        def _():
            for copy in copies:
                getattr(copy, action)()

    fine_corner = [
        remote(12 + 2 * n + m, sides.at[n, source], sides.at[n, target], device)
        for n in range(2)
        for m, (source, target, device) in enumerate(
            (
                (slice(PAD + EDGE - CORNER, PAD + EDGE), slice(PAD - CORNER, PAD), (down, lon)),
                (slice(PAD, PAD + CORNER), slice(PAD + EDGE, PAD + EDGE + CORNER), (up, lon)),
            )
        )
    ]
    base = CH * CW
    first_row, last_row = atts.at[0:CW], atts.at[base - CW : base]
    att_moves = [
        remote(16 + n, source, atts.at[base + 8 * n : base + 8 * n + 8], device)
        for n, (source, device) in enumerate(
            (
                (edges.at[8:16], (lat, right)),
                (edges.at[0:8], (lat, left)),
                (last_row, (down, lon)),
                (first_row, (up, lon)),
                (last_row, (down, right)),
                (last_row, (down, left)),
                (first_row, (up, right)),
                (first_row, (up, left)),
            )
        )
    ]

    pl.semaphore_wait(barrier, jnp.where(linked, 10, 8))

    for copy in coarse_lon:
        copy.start()
    when_down("start", coarse_lat[0], cap_down)
    when_up("start", coarse_lat[1], cap_up)

    loads[0].wait()
    cell, place = iota((EDGE, FH * 8), 0), iota((EDGE, FH * 8), 1)
    for n in range(2):
        wanted = cell // RADIUS * 8 + cell % RADIUS + 2 * n
        pick = jnp.where(place == wanted, 1.0, 0.0).astype(BF16)
        outer = own[:, n * (FW - 8) : n * (FW - 8) + 8, :]
        packed[n] = dot(pick, flat(outer)).astype(BF16)

    for n in range(2):
        for low in (0, PAD + EDGE + CORNER):
            sides[n, low : low + PAD - CORNER] = jnp.zeros((PAD - CORNER, 2 * D), BF16)

    def clear(pole):
        gone = slice(2 * CH * pole, 2 * CH * pole + CH)
        cext[gone] = jnp.zeros((CH, 3 * CW, 2 * D), BF16)
        caps[pole] = jnp.zeros((RADIUS, FW, 2 * D), BF16)
        gone = slice(PAD + EDGE, PAD + EDGE + CORNER) if pole else slice(PAD - CORNER, PAD)
        for n in range(2):
            sides[n, gone] = jnp.zeros((CORNER, 2 * D), BF16)
        for group in (2, 4, 5) if not pole else (3, 6, 7):
            place = CH * CW + 8 * group
            atts[place : place + 8] = jnp.zeros((8, D), BF16)

    @pl.when(lat == 0)
    def _():
        clear(0)

    @pl.when(lat == lats - 1)
    def _():
        clear(1)

    pos = iota((CELLS, 1), 0)
    own_marks[0] = query_marks(pos // FW, pos % FW, CELLS)
    own_marks[1] = key_marks(pos // FW, pos % FW, CELLS, 0, FH)
    pos = iota((SIDE, 1), 0) + (6 * 10 - PAD)
    for n in range(2):
        side_marks[n] = key_marks(
            pos // 6 - 10, pos % 6 + (FW if n else -RADIUS), SIDE, lat * FH, lats * FH
        )
    pos = iota((CAP, 1), 0)
    for n in range(2):
        cap_marks[n] = key_marks(
            pos // FW + (FH if n else -RADIUS), pos % FW, CAP, lat * FH, lats * FH
        )
    lane = iota((1, CYCLE), 1)
    table[...] = spread(lane // (3 * CW) - 1, lane % (3 * CW) - CW, lat, lats)
    table2[...] = spread(*att_places(), lat, lats)

    first = iota((1, 128), 1) < 64

    def heads(query, scale):
        low = jnp.where(first, scale, 0.0).astype(BF16)
        high = jnp.where(first, 0.0, scale).astype(BF16)
        return query * low, query * high

    def lanes_of(pair, offset=0):
        return pl.ds(pair * 128 + offset, 128)

    def over_pairs(part):
        for pair in range(4):
            part(pair, 0)

    def own_part(pair, carry):
        lanes, vlanes = lanes_of(pair), lanes_of(pair, D)
        for block in range(3):
            rows = slice(8 * block, 8 * block + 8)
            low, high = max(8 * block - RADIUS, 0), min(8 * block + 8 + RADIUS, FH)
            count = (high - low) * FW
            query = fq[rows, :, lanes].reshape(8 * FW, 128)
            keys = jnp.concatenate(
                [own[low:high, :, lanes].reshape(count, 128), own_marks[1, low * FW : high * FW]],
                1,
            )
            values = jnp.concatenate(
                [own[low:high, :, vlanes].reshape(count, 128), jnp.ones((count, 128), BF16)], 1
            )
            marks = own_marks[0, 8 * block * FW : (8 * block + 8) * FW]
            found = attend(heads(query, 0.125), marks, keys, values)
            for ref, value in zip((total, weight, largest), found):
                ref[rows, :, lanes] = value.reshape(8, FW, 128)
        return carry

    loads[2].wait()
    for pair in (0, 1):
        own_part(pair, 0)
    for copy in coarse_lon:
        copy.wait_recv()
    when_down("start", *coarse_corner[0::2])
    when_up("start", *coarse_corner[1::2])

    for copy in fine_lon:
        copy.start()

    @pl.when(relay)
    def _():
        relayed.wait_recv()
        cap_on.start()

    for pair in (2, 3):
        own_part(pair, 0)
    when_up("wait_recv", coarse_lat[0], *coarse_corner[0::2])
    when_down("wait_recv", coarse_lat[1], *coarse_corner[1::2])
    loads[1].wait()
    loads[3].wait()

    cflat[...] = flat(cext[...])
    pos = iota((CH * CW, 1), 0)
    cq_marks = query_marks(pos // CW, pos % CW, CH * CW)
    pos = iota((CKEYS, 1), 0)
    ckey_marks = key_marks(
        pos // (3 * CW) - CH, pos % (3 * CW) - CW, CKEYS, lat * CH, lats * CH
    )
    for pair in range(4):
        lanes, vlanes = lanes_of(pair), lanes_of(pair, D)
        keys = jnp.concatenate([cflat[:, lanes], ckey_marks], 1)
        values = jnp.concatenate([cflat[:, vlanes], jnp.ones((CKEYS, 128), BF16)], 1)
        found = attend(
            heads(flat(cq[:, :, lanes]), 0.125), cq_marks, keys, values, stack=True
        )
        atts[0:base, lanes] = (found[0] / found[1]).astype(BF16)
    row, col = iota((16, base), 0), iota((16, base), 1)
    wanted = row % 8 * CW + jnp.where(row < 8, 0, CW - 1)
    pick = jnp.where((col == wanted) & (row % 8 < CH), 1.0, 0.0).astype(BF16)
    edges[...] = dot(pick, atts[0:base]).astype(BF16)
    att_lon = att_moves[0:2]
    att_down, att_up = att_moves[2:3] + att_moves[4:6], att_moves[3:4] + att_moves[6:8]
    for copy in att_lon:
        copy.start()
    when_down("start", *att_down)
    when_up("start", *att_up)

    start = (CH - 1) * 3 * CW
    for part in range(4):
        lanes = slice(part * 256, part * 256 + 256)
        upkv[:, lanes] = dot(table[...], cflat[start : start + CYCLE, lanes]).astype(BF16)

    def cross_part(pair, carry):
        lanes, vlanes = lanes_of(pair), lanes_of(pair, D)
        query = fq[:, :, lanes].reshape(CELLS, 128).astype(F32) * (0.125 * LOG2E)
        main = query.astype(BF16)
        rest = (query - main.astype(F32)).astype(BF16)
        heads_of = [
            jnp.concatenate([a, b], 1) for a, b in zip(heads(main, 1.0), heads(rest, 1.0))
        ]
        keys = jnp.concatenate([upkv[:, lanes], upkv[:, lanes]], 1)
        values = jnp.concatenate([upkv[:, vlanes], jnp.ones((CELLS, 128), BF16)], 1)
        found = attend(heads_of, None, keys, values, True)
        acc[:, :, lanes] = (found[0] / found[1]).reshape(FH, FW, 128)
        return carry

    over_pairs(cross_part)

    for copy in fine_lon:
        copy.wait_recv()
    when_down("start", *fine_corner[0::2])
    when_up("start", *fine_corner[1::2])
    when_up("wait_recv", cap_from[0])
    when_down("wait_recv", cap_from[1])

    def halo_part(rows, cols, shape, marks, halo, halo_marks, count, pair):
        lanes, vlanes = lanes_of(pair), lanes_of(pair, D)
        query = flat(fq[rows, cols, lanes])
        keys = jnp.concatenate([halo[..., lanes].reshape(count, 128), halo_marks], 1)
        values = jnp.concatenate([halo[..., vlanes].reshape(count, 128), jnp.ones((count, 128), BF16)], 1)
        value, amount, top = attend(heads(query, 0.125), marks, keys, values, stack=True)
        old = largest[rows, cols, lanes].reshape(-1, 128)
        new = jnp.maximum(old, top)
        keep, add = jnp.exp(old - new), jnp.exp(top - new)
        largest[rows, cols, lanes] = new.reshape(shape)
        for ref, part in ((total, value), (weight, amount)):
            before = ref[rows, cols, lanes].reshape(-1, 128)
            ref[rows, cols, lanes] = (before * keep + part * add).reshape(shape)

    def cap_part(pair, carry):
        for n in range(2):
            low = n * (FH - RADIUS)
            marks = own_marks[0, low * FW : (low + RADIUS) * FW]
            halo_part(
                slice(low, low + RADIUS), slice(0, FW), (RADIUS, FW, 128), marks,
                caps.at[n], cap_marks[n], CAP, pair,
            )
        return carry

    over_pairs(cap_part)

    loads[4].wait()
    for copy in att_lon:
        copy.wait_recv()
    when_up("wait_recv", *att_down)
    when_down("wait_recv", *att_up)
    acc[...] += dot(table2[...], atts[...]).reshape(FH, FW, D)
    when_up("wait_recv", *fine_corner[0::2])
    when_down("wait_recv", *fine_corner[1::2])

    pos = iota((FH * 8, 1), 0)
    outer_marks = [query_marks(pos // 8, pos % 8 + n * (FW - 8), FH * 8) for n in range(2)]

    def side_part(pair, carry):
        for n in range(2):
            low = n * (FW - 8)
            halo_part(
                slice(0, FH), slice(low, low + 8), (FH, 8, 128), outer_marks[n],
                sides.at[n], side_marks[n], SIDE, pair,
            )
        return carry

    over_pairs(side_part)

    fine = (total[...] / weight[...]).astype(BF16).astype(F32)
    joined = (fine + acc[...]).astype(BF16).reshape(CELLS, D)
    outv[...] = dot(joined, w[...]).astype(BF16).reshape(FH, FW, D)
    store = pltpu.make_async_copy(outv, out_hbm, osem)
    store.start()
    for copy in coarse_lon + fine_lon + att_lon:
        copy.wait_send()
    when_down(
        "wait_send", coarse_lat[0], cap_down, *coarse_corner[0::2], *fine_corner[0::2], *att_down
    )
    when_up(
        "wait_send", coarse_lat[1], cap_up, *coarse_corner[1::2], *fine_corner[1::2], *att_up
    )

    @pl.when(relay)
    def _():
        cap_on.wait_send()

    store.wait()


def shards(fine_query, fine_keyval, coarse_query, coarse_keyval, out_weight):
    lats, lons = lax.axis_size("lat"), lax.axis_size("lon")
    anywhere = pl.BlockSpec(memory_space=pl.ANY)
    dma, vmem = pltpu.SemaphoreType.DMA, pltpu.VMEM
    return pl.pallas_call(
        functools.partial(kernel, lats, lons),
        out_shape=jax.ShapeDtypeStruct(fine_query.shape, BF16),
        in_specs=[anywhere] * 5,
        out_specs=anywhere,
        scratch_shapes=[
            vmem((FH, FW, D), BF16),
            vmem((FH, FW, 2 * D), BF16),
            vmem((CH, CW, D), BF16),
            vmem((3 * CH, 3 * CW, 2 * D), BF16),
            vmem((D, D), BF16),
            vmem((2, EDGE, 2 * D), BF16),
            vmem((2, SIDE, 2 * D), BF16),
            vmem((3, RADIUS, FW, 2 * D), BF16),
            vmem((CKEYS, 2 * D), BF16),
            vmem((ATTS, D), BF16),
            vmem((16, D), BF16),
            vmem((CELLS, CYCLE), BF16),
            vmem((CELLS, ATTS), BF16),
            vmem((CELLS, 2 * D), BF16),
            vmem((2, CELLS, 128), BF16),
            vmem((2, SIDE, 128), BF16),
            vmem((2, CAP, 128), BF16),
            vmem((FH, FW, D), F32),
            vmem((FH, FW, D), F32),
            vmem((FH, FW, D), F32),
            vmem((FH, FW, D), F32),
            vmem((FH, FW, D), BF16),
            dma((5,)),
            dma((25,)),
            dma((25,)),
            dma,
        ],
        compiler_params=pltpu.CompilerParams(
            collective_id=0, has_side_effects=True, vmem_limit_bytes=56 << 20
        ),
        name="neighbourhood",
    )(fine_query, fine_keyval, coarse_query, coarse_keyval, out_weight)


def solution(mesh):
    tile = P("lat", "lon", None)
    return jax.shard_map(
        shards, mesh=mesh, in_specs=(tile, tile, tile, tile, P()), out_specs=tile,
        check_vma=False,
    )
```

```python
import functools

import jax
import jax.numpy as jnp
from jax import lax
from jax.experimental import pallas as pl
from jax.experimental.pallas import tpu as pltpu
from jax.sharding import PartitionSpec as P

RADIUS = 6
FH, FW, CH, CW, D = 24, 32, 6, 8, 512
CELLS = FH * FW
EDGE = FH * RADIUS
CORNER = 40
PAD = 56
SIDE = EDGE + 2 * PAD
CAP = RADIUS * FW
CKEYS = 3 * CH * 3 * CW
CYCLE = (CH + 2) * 3 * CW
ATTS = CH * CW + 64
BIG = 2.0**100
LOG2E = 1.4426950408889634
MESH = pl.DeviceIdType.MESH
F32, BF16 = jnp.float32, jnp.bfloat16


def iota(shape, dim):
    return lax.broadcasted_iota(jnp.int32, shape, dim)


def dot_nt(a, b):
    return lax.dot_general(a, b, (((1,), (1,)), ((), ())), preferred_element_type=F32)


def dot(a, b):
    return jnp.dot(a, b, preferred_element_type=F32)


def flat(block):
    return block.astype(F32).reshape(-1, block.shape[-1]).astype(BF16)


def query_marks(row, col, count):
    lane = iota((count, 128), 1)
    hit = (lane == row) | (lane == col + 32) | (lane == 64)
    return jnp.where(hit, 1.0, 0.0).astype(BF16)


def key_marks(row, col, count, first_row, row_count):
    lane = iota((count, 128), 1)
    row_out = (lane < 24) & (jnp.abs(row - lane) > RADIUS)
    col_out = (lane >= 32) & (lane < 64) & (jnp.abs(col - lane + 32) > RADIUS)
    place = row + first_row
    bad = (lane == 64) & ((place < 0) | (place >= row_count))
    return jnp.where(row_out | col_out | bad, -BIG, 0.0).astype(BF16)


def attend(query, marks, keys, values, base2=False, stack=False):
    parts = []
    if marks is not None:
        query = [jnp.concatenate([head, marks], 1) for head in query]
    for head in [jnp.concatenate(query, 0)] if stack else query:
        scores = dot_nt(head, keys)
        top = jnp.max(scores, axis=1, keepdims=True)
        raised = jnp.exp2(scores - top) if base2 else jnp.exp(scores - top)
        both = dot(raised.astype(BF16), values)
        parts.append((both[:, :128], both[:, 128:], top))
    first = iota((1, 128), 1) < 64
    if stack:
        half = query[0].shape[0]
        parts = [[x[:half] for x in parts[0]], [x[half:] for x in parts[0]]]
    return [jnp.where(first, low, high) for low, high in zip(*parts)]


def hat(x, place):
    return jnp.maximum(1.0 - jnp.abs(x - place), 0.0)


def spread(a, b, lat, lats):
    pos = iota((CELLS, 1), 0)
    x = ((pos // FW).astype(F32) - 1.5) / 4.0
    x = jnp.maximum(x, jnp.where(lat == 0, 0.0, -1.0))
    x = jnp.minimum(x, jnp.where(lat == lats - 1, CH - 1.0, CH + 0.0))
    y = ((pos % FW).astype(F32) - 1.5) / 4.0
    return (hat(x, a.astype(F32)) * hat(y, b.astype(F32))).astype(BF16)


def att_places():
    n = iota((1, ATTS), 1)
    a, b = n // CW, n % CW
    group, k = n // 8, n % 8
    far = -100
    a = jnp.where((group == 6) | (group == 7), jnp.where(k < CH, k, far), a)
    b = jnp.where(group == 6, -1, jnp.where(group == 7, CW, b))
    a = jnp.where(group == 8, -1, jnp.where(group == 9, CH, a))
    a = jnp.where((group == 10) | (group == 11), -1, a)
    a = jnp.where((group == 12) | (group == 13), CH, a)
    b = jnp.where((group == 10) | (group == 12), jnp.where(k == CW - 1, -1, far), b)
    b = jnp.where((group == 11) | (group == 13), jnp.where(k == 0, CW, far), b)
    return a, b


def kernel(
    lats, lons, fq_hbm, fkv_hbm, cq_hbm, ckv_hbm, out_hbm,
    fq, own, cq, cext, packed, sides, caps, cflat, atts, edges, table, table2, upkv,
    own_marks, side_marks, cap_marks, total, weight, largest, acc, outv,
    local, send, recv, osem,
):
    lat, lon = lax.axis_index("lat"), lax.axis_index("lon")
    up, down = lax.rem(lat + lats - 1, lats), lax.rem(lat + 1, lats)
    left, right = lax.rem(lon + lons - 1, lons), lax.rem(lon + 1, lons)

    loads = [
        pltpu.make_async_copy(fkv_hbm, own, local.at[0]),
        pltpu.make_async_copy(ckv_hbm, cext.at[CH : 2 * CH, CW : 2 * CW], local.at[1]),
        pltpu.make_async_copy(fq_hbm, fq, local.at[2]),
        pltpu.make_async_copy(cq_hbm, cq, local.at[3]),
    ]
    for load in loads:
        load.start()

    barrier = pltpu.get_barrier_semaphore()
    for other in (
        (up, lon), (down, lon), (lat, left), (lat, right),
        (up, left), (up, right), (down, left), (down, right),
    ):
        pl.semaphore_signal(barrier, inc=1, device_id=other, device_id_type=MESH)
    middle = lats // 2
    not_top, not_last = lat != 0, lat != lats - 1
    relay = (lat == 0) | (lat == lats - 1)
    linked = relay | (lat == middle - 1) | (lat == middle)
    across = lax.rem(lat + middle, lats)
    beside = jnp.where(lat < middle, middle - 1 - lat, lats + middle - 1 - lat)

    @pl.when(linked)
    def _():
        for other in (across, beside):
            pl.semaphore_signal(barrier, inc=1, device_id=(other, lon), device_id_type=MESH)

    def remote(number, source, target, device):
        return pltpu.make_async_remote_copy(
            src_ref=source, dst_ref=target, send_sem=send.at[number],
            recv_sem=recv.at[number], device_id=device, device_id_type=MESH,
        )

    mid = slice(CH, 2 * CH)
    west, centre, east = slice(0, CW), slice(CW, 2 * CW), slice(2 * CW, 3 * CW)
    coarse_lon = [
        remote(0, ckv_hbm, cext.at[mid, west], (lat, right)),
        remote(1, ckv_hbm, cext.at[mid, east], (lat, left)),
    ]
    coarse_lat = [
        remote(2, ckv_hbm, cext.at[0:CH, centre], (down, lon)),
        remote(3, ckv_hbm, cext.at[2 * CH : 3 * CH, centre], (up, lon)),
    ]
    coarse_corner = [
        remote(4 + 2 * n + m, cext.at[mid, side], cext.at[rows, side], device)
        for n, side in enumerate((west, east))
        for m, (rows, device) in enumerate(
            ((slice(0, CH), (down, lon)), (slice(2 * CH, 3 * CH), (up, lon)))
        )
    ]
    def strip_moves(number, low, high):
        source, target = slice(low, high), slice(PAD + low, PAD + high)
        return [
            remote(number, packed.at[1, source], sides.at[0, target], (lat, right)),
            remote(number + 1, packed.at[0, source], sides.at[1, target], (lat, left)),
        ]

    ends_lon = strip_moves(8, 0, CORNER) + strip_moves(25, EDGE - CORNER, EDGE)
    rest_lon = strip_moves(27, CORNER, EDGE - CORNER)
    via_top, via_last = lat == middle - 1, lat == middle

    def cap_move(number, arrival, source, slot, device):
        return pltpu.make_async_remote_copy(
            src_ref=source, dst_ref=caps.at[slot], send_sem=send.at[number],
            recv_sem=recv.at[arrival], device_id=(device, lon), device_id_type=MESH,
        )

    cap_down = cap_move(
        10, jnp.where(via_top, 24, 10), fkv_hbm.at[FH - RADIUS : FH],
        jnp.where(via_top, 2, 0), jnp.where(via_top, 0, down),
    )
    cap_up = cap_move(
        11, jnp.where(via_last, 24, 11), fkv_hbm.at[0:RADIUS],
        jnp.where(via_last, 2, 1), jnp.where(via_last, lats - 1, up),
    )
    cap_on = cap_move(
        24, jnp.where(lat == 0, 10, 11), caps.at[2],
        jnp.where(lat == 0, 0, 1), jnp.where(lat == 0, middle, middle - 1),
    )
    relayed = remote(24, fkv_hbm.at[0:RADIUS], caps.at[2], (lat, right))
    cap_from = [
        remote(10, fkv_hbm.at[0:RADIUS], caps.at[0], (lat, right)),
        remote(11, fkv_hbm.at[0:RADIUS], caps.at[1], (lat, right)),
    ]

    def when_down(action, *copies):
        @pl.when(not_last)
        def _():
            for copy in copies:
                getattr(copy, action)()

    def when_up(action, *copies):
        @pl.when(not_top)
        def _():
            for copy in copies:
                getattr(copy, action)()

    fine_corner = [
        remote(12 + 2 * n + m, sides.at[n, source], sides.at[n, target], device)
        for n in range(2)
        for m, (source, target, device) in enumerate(
            (
                (slice(PAD + EDGE - CORNER, PAD + EDGE), slice(PAD - CORNER, PAD), (down, lon)),
                (slice(PAD, PAD + CORNER), slice(PAD + EDGE, PAD + EDGE + CORNER), (up, lon)),
            )
        )
    ]
    base = CH * CW
    first_row, last_row = atts.at[0:CW], atts.at[base - CW : base]
    att_moves = [
        remote(16 + n, source, atts.at[base + 8 * n : base + 8 * n + 8], device)
        for n, (source, device) in enumerate(
            (
                (edges.at[8:16], (lat, right)),
                (edges.at[0:8], (lat, left)),
                (last_row, (down, lon)),
                (first_row, (up, lon)),
                (last_row, (down, right)),
                (last_row, (down, left)),
                (first_row, (up, right)),
                (first_row, (up, left)),
            )
        )
    ]

    pl.semaphore_wait(barrier, jnp.where(linked, 10, 8))

    for copy in coarse_lon:
        copy.start()
    when_down("start", coarse_lat[0], cap_down)
    when_up("start", coarse_lat[1], cap_up)

    loads[0].wait()
    cell, place = iota((EDGE, FH * 8), 0), iota((EDGE, FH * 8), 1)
    for n in range(2):
        wanted = cell // RADIUS * 8 + cell % RADIUS + 2 * n
        pick = jnp.where(place == wanted, 1.0, 0.0).astype(BF16)
        outer = own[:, n * (FW - 8) : n * (FW - 8) + 8, :]
        packed[n] = dot(pick, flat(outer)).astype(BF16)

    for n in range(2):
        for low in (0, PAD + EDGE + CORNER):
            sides[n, low : low + PAD - CORNER] = jnp.zeros((PAD - CORNER, 2 * D), BF16)

    def clear(pole):
        gone = slice(2 * CH * pole, 2 * CH * pole + CH)
        cext[gone] = jnp.zeros((CH, 3 * CW, 2 * D), BF16)
        caps[pole] = jnp.zeros((RADIUS, FW, 2 * D), BF16)
        gone = slice(PAD + EDGE, PAD + EDGE + CORNER) if pole else slice(PAD - CORNER, PAD)
        for n in range(2):
            sides[n, gone] = jnp.zeros((CORNER, 2 * D), BF16)
        for group in (2, 4, 5) if not pole else (3, 6, 7):
            place = CH * CW + 8 * group
            atts[place : place + 8] = jnp.zeros((8, D), BF16)

    @pl.when(lat == 0)
    def _():
        clear(0)

    @pl.when(lat == lats - 1)
    def _():
        clear(1)

    pos = iota((CELLS, 1), 0)
    own_marks[0] = query_marks(pos // FW, pos % FW, CELLS)
    own_marks[1] = key_marks(pos // FW, pos % FW, CELLS, 0, FH)
    pos = iota((SIDE, 1), 0) + (6 * 10 - PAD)
    for n in range(2):
        side_marks[n] = key_marks(
            pos // 6 - 10, pos % 6 + (FW if n else -RADIUS), SIDE, lat * FH, lats * FH
        )
    pos = iota((CAP, 1), 0)
    for n in range(2):
        cap_marks[n] = key_marks(
            pos // FW + (FH if n else -RADIUS), pos % FW, CAP, lat * FH, lats * FH
        )
    lane = iota((1, CYCLE), 1)
    table[...] = spread(lane // (3 * CW) - 1, lane % (3 * CW) - CW, lat, lats)
    table2[...] = spread(*att_places(), lat, lats)

    first = iota((1, 128), 1) < 64

    def heads(query, scale):
        low = jnp.where(first, scale, 0.0).astype(BF16)
        high = jnp.where(first, 0.0, scale).astype(BF16)
        return query * low, query * high

    def lanes_of(pair, offset=0):
        return pl.ds(pair * 128 + offset, 128)

    def over_pairs(part):
        for pair in range(4):
            part(pair, 0)

    def own_part(pair, carry):
        lanes, vlanes = lanes_of(pair), lanes_of(pair, D)
        for block in range(3):
            rows = slice(8 * block, 8 * block + 8)
            low, high = max(8 * block - RADIUS, 0), min(8 * block + 8 + RADIUS, FH)
            count = (high - low) * FW
            query = fq[rows, :, lanes].reshape(8 * FW, 128)
            keys = jnp.concatenate(
                [own[low:high, :, lanes].reshape(count, 128), own_marks[1, low * FW : high * FW]],
                1,
            )
            values = jnp.concatenate(
                [own[low:high, :, vlanes].reshape(count, 128), jnp.ones((count, 128), BF16)], 1
            )
            marks = own_marks[0, 8 * block * FW : (8 * block + 8) * FW]
            found = attend(heads(query, 0.125), marks, keys, values)
            for ref, value in zip((total, weight, largest), found):
                ref[rows, :, lanes] = value.reshape(8, FW, 128)
        return carry

    loads[2].wait()
    for pair in (0, 1):
        own_part(pair, 0)
    for copy in coarse_lon:
        copy.wait_recv()
    when_down("start", *coarse_corner[0::2])
    when_up("start", *coarse_corner[1::2])

    @pl.when(relay)
    def _():
        relayed.wait_recv()
        cap_on.start()

    for copy in ends_lon + rest_lon:
        copy.start()

    for pair in (2, 3):
        own_part(pair, 0)
    when_up("wait_recv", coarse_lat[0], *coarse_corner[0::2])
    when_down("wait_recv", coarse_lat[1], *coarse_corner[1::2])
    loads[1].wait()
    loads[3].wait()

    cflat[...] = flat(cext[...])
    pos = iota((CH * CW, 1), 0)
    cq_marks = query_marks(pos // CW, pos % CW, CH * CW)
    pos = iota((CKEYS, 1), 0)
    ckey_marks = key_marks(
        pos // (3 * CW) - CH, pos % (3 * CW) - CW, CKEYS, lat * CH, lats * CH
    )
    for pair in range(4):
        lanes, vlanes = lanes_of(pair), lanes_of(pair, D)
        keys = jnp.concatenate([cflat[:, lanes], ckey_marks], 1)
        values = jnp.concatenate([cflat[:, vlanes], jnp.ones((CKEYS, 128), BF16)], 1)
        found = attend(
            heads(flat(cq[:, :, lanes]), 0.125), cq_marks, keys, values, stack=True
        )
        atts[0:base, lanes] = (found[0] / found[1]).astype(BF16)
    row, col = iota((16, base), 0), iota((16, base), 1)
    wanted = row % 8 * CW + jnp.where(row < 8, 0, CW - 1)
    pick = jnp.where((col == wanted) & (row % 8 < CH), 1.0, 0.0).astype(BF16)
    edges[...] = dot(pick, atts[0:base]).astype(BF16)
    att_lon = att_moves[0:2]
    att_down, att_up = att_moves[2:3] + att_moves[4:6], att_moves[3:4] + att_moves[6:8]
    for copy in att_lon:
        copy.start()
    when_down("start", *att_down)
    when_up("start", *att_up)

    start = (CH - 1) * 3 * CW
    for part in range(4):
        lanes = slice(part * 256, part * 256 + 256)
        upkv[:, lanes] = dot(table[...], cflat[start : start + CYCLE, lanes]).astype(BF16)

    def cross_part(pair, carry):
        lanes, vlanes = lanes_of(pair), lanes_of(pair, D)
        query = fq[:, :, lanes].reshape(CELLS, 128).astype(F32) * (0.125 * LOG2E)
        main = query.astype(BF16)
        rest = (query - main.astype(F32)).astype(BF16)
        heads_of = [
            jnp.concatenate([a, b], 1) for a, b in zip(heads(main, 1.0), heads(rest, 1.0))
        ]
        keys = jnp.concatenate([upkv[:, lanes], upkv[:, lanes]], 1)
        values = jnp.concatenate([upkv[:, vlanes], jnp.ones((CELLS, 128), BF16)], 1)
        found = attend(heads_of, None, keys, values, True)
        acc[:, :, lanes] = (found[0] / found[1]).reshape(FH, FW, 128)
        return carry

    for pair in (0, 1):
        cross_part(pair, 0)
    for copy in ends_lon:
        copy.wait_recv()
    when_down("start", *fine_corner[0::2])
    when_up("start", *fine_corner[1::2])
    for pair in (2, 3):
        cross_part(pair, 0)

    when_up("wait_recv", cap_from[0])
    when_down("wait_recv", cap_from[1])

    def halo_part(rows, cols, shape, marks, halo, halo_marks, count, pair):
        lanes, vlanes = lanes_of(pair), lanes_of(pair, D)
        query = flat(fq[rows, cols, lanes])
        keys = jnp.concatenate([halo[..., lanes].reshape(count, 128), halo_marks], 1)
        values = jnp.concatenate([halo[..., vlanes].reshape(count, 128), jnp.ones((count, 128), BF16)], 1)
        value, amount, top = attend(heads(query, 0.125), marks, keys, values, stack=True)
        old = largest[rows, cols, lanes].reshape(-1, 128)
        new = jnp.maximum(old, top)
        keep, add = jnp.exp(old - new), jnp.exp(top - new)
        largest[rows, cols, lanes] = new.reshape(shape)
        for ref, part in ((total, value), (weight, amount)):
            before = ref[rows, cols, lanes].reshape(-1, 128)
            ref[rows, cols, lanes] = (before * keep + part * add).reshape(shape)

    def cap_part(pair, carry):
        for n in range(2):
            low = n * (FH - RADIUS)
            marks = own_marks[0, low * FW : (low + RADIUS) * FW]
            halo_part(
                slice(low, low + RADIUS), slice(0, FW), (RADIUS, FW, 128), marks,
                caps.at[n], cap_marks[n], CAP, pair,
            )
        return carry

    over_pairs(cap_part)

    for copy in att_lon:
        copy.wait_recv()
    when_up("wait_recv", *att_down)
    when_down("wait_recv", *att_up)
    acc[...] += dot(table2[...], atts[...]).reshape(FH, FW, D)
    for copy in rest_lon:
        copy.wait_recv()
    when_up("wait_recv", *fine_corner[0::2])
    when_down("wait_recv", *fine_corner[1::2])

    pos = iota((FH * 8, 1), 0)
    outer_marks = [query_marks(pos // 8, pos % 8 + n * (FW - 8), FH * 8) for n in range(2)]

    def side_part(pair, carry):
        for n in range(2):
            low = n * (FW - 8)
            halo_part(
                slice(0, FH), slice(low, low + 8), (FH, 8, 128), outer_marks[n],
                sides.at[n], side_marks[n], SIDE, pair,
            )
        return carry

    over_pairs(side_part)

    fine = (total[...] / weight[...]).astype(BF16).astype(F32)
    outv[...] = (fine + acc[...]).astype(BF16)
    store = pltpu.make_async_copy(outv, out_hbm, osem)
    store.start()
    for copy in coarse_lon + ends_lon + rest_lon + att_lon:
        copy.wait_send()
    when_down(
        "wait_send", coarse_lat[0], cap_down, *coarse_corner[0::2], *fine_corner[0::2], *att_down
    )
    when_up(
        "wait_send", coarse_lat[1], cap_up, *coarse_corner[1::2], *fine_corner[1::2], *att_up
    )

    @pl.when(relay)
    def _():
        cap_on.wait_send()

    store.wait()


def shards(fine_query, fine_keyval, coarse_query, coarse_keyval, out_weight):
    lats, lons = lax.axis_size("lat"), lax.axis_size("lon")
    anywhere = pl.BlockSpec(memory_space=pl.ANY)
    dma, vmem = pltpu.SemaphoreType.DMA, pltpu.VMEM
    joined = pl.pallas_call(
        functools.partial(kernel, lats, lons),
        out_shape=jax.ShapeDtypeStruct(fine_query.shape, BF16),
        in_specs=[anywhere] * 4,
        out_specs=anywhere,
        scratch_shapes=[
            vmem((FH, FW, D), BF16),
            vmem((FH, FW, 2 * D), BF16),
            vmem((CH, CW, D), BF16),
            vmem((3 * CH, 3 * CW, 2 * D), BF16),
            vmem((2, EDGE, 2 * D), BF16),
            vmem((2, SIDE, 2 * D), BF16),
            vmem((3, RADIUS, FW, 2 * D), BF16),
            vmem((CKEYS, 2 * D), BF16),
            vmem((ATTS, D), BF16),
            vmem((16, D), BF16),
            vmem((CELLS, CYCLE), BF16),
            vmem((CELLS, ATTS), BF16),
            vmem((CELLS, 2 * D), BF16),
            vmem((2, CELLS, 128), BF16),
            vmem((2, SIDE, 128), BF16),
            vmem((2, CAP, 128), BF16),
            vmem((FH, FW, D), F32),
            vmem((FH, FW, D), F32),
            vmem((FH, FW, D), F32),
            vmem((FH, FW, D), F32),
            vmem((FH, FW, D), BF16),
            dma((4,)),
            dma((29,)),
            dma((29,)),
            dma,
        ],
        compiler_params=pltpu.CompilerParams(
            collective_id=0, has_side_effects=True, vmem_limit_bytes=56 << 20
        ),
        name="neighbourhood",
    )(fine_query, fine_keyval, coarse_query, coarse_keyval)
    return dot(joined, out_weight).astype(BF16)


def solution(mesh):
    tile = P("lat", "lon", None)
    return jax.shard_map(
        shards, mesh=mesh, in_specs=(tile, tile, tile, tile, P()), out_specs=tile,
        check_vma=False,
    )
```

```python
import functools

import jax
import jax.numpy as jnp
from jax import lax
from jax.experimental import pallas as pl
from jax.experimental.pallas import tpu as pltpu
from jax.sharding import PartitionSpec as P

RADIUS = 6
FH, FW, CH, CW, D = 24, 32, 6, 8, 512
CELLS = FH * FW
EDGE = FH * RADIUS
CORNER = 40
PAD = 56
SIDE = EDGE + 2 * PAD
CAP = RADIUS * FW
CKEYS = 3 * CH * 3 * CW
CYCLE = (CH + 2) * 3 * CW
ATTS = CH * CW + 64
BIG = 2.0**100
LOG2E = 1.4426950408889634
MESH = pl.DeviceIdType.MESH
F32, BF16 = jnp.float32, jnp.bfloat16


def iota(shape, dim):
    return lax.broadcasted_iota(jnp.int32, shape, dim)


def dot_nt(a, b):
    return lax.dot_general(a, b, (((1,), (1,)), ((), ())), preferred_element_type=F32)


def dot(a, b):
    return jnp.dot(a, b, preferred_element_type=F32)


def flat(block):
    return block.astype(F32).reshape(-1, block.shape[-1]).astype(BF16)


def query_marks(row, col, count):
    lane = iota((count, 128), 1)
    hit = (lane == row) | (lane == col + 32) | (lane == 64)
    return jnp.where(hit, 1.0, 0.0).astype(BF16)


def key_marks(row, col, count, first_row, row_count):
    lane = iota((count, 128), 1)
    row_out = (lane < 24) & (jnp.abs(row - lane) > RADIUS)
    col_out = (lane >= 32) & (lane < 64) & (jnp.abs(col - lane + 32) > RADIUS)
    place = row + first_row
    bad = (lane == 64) & ((place < 0) | (place >= row_count))
    return jnp.where(row_out | col_out | bad, -BIG, 0.0).astype(BF16)


def attend(query, marks, keys, values, base2=False, stack=False):
    parts = []
    if marks is not None:
        query = [jnp.concatenate([head, marks], 1) for head in query]
    for head in [jnp.concatenate(query, 0)] if stack else query:
        scores = dot_nt(head, keys)
        top = jnp.max(scores, axis=1, keepdims=True)
        raised = jnp.exp2(scores - top) if base2 else jnp.exp(scores - top)
        both = dot(raised.astype(BF16), values)
        parts.append((both[:, :128], both[:, 128:], top))
    first = iota((1, 128), 1) < 64
    if stack:
        half = query[0].shape[0]
        parts = [[x[:half] for x in parts[0]], [x[half:] for x in parts[0]]]
    return [jnp.where(first, low, high) for low, high in zip(*parts)]


def hat(x, place):
    return jnp.maximum(1.0 - jnp.abs(x - place), 0.0)


def spread(a, b, lat, lats):
    pos = iota((CELLS, 1), 0)
    x = ((pos // FW).astype(F32) - 1.5) / 4.0
    x = jnp.maximum(x, jnp.where(lat == 0, 0.0, -1.0))
    x = jnp.minimum(x, jnp.where(lat == lats - 1, CH - 1.0, CH + 0.0))
    y = ((pos % FW).astype(F32) - 1.5) / 4.0
    return (hat(x, a.astype(F32)) * hat(y, b.astype(F32))).astype(BF16)


def att_places():
    n = iota((1, ATTS), 1)
    a, b = n // CW, n % CW
    group, k = n // 8, n % 8
    far = -100
    a = jnp.where((group == 6) | (group == 7), jnp.where(k < CH, k, far), a)
    b = jnp.where(group == 6, -1, jnp.where(group == 7, CW, b))
    a = jnp.where(group == 8, -1, jnp.where(group == 9, CH, a))
    a = jnp.where((group == 10) | (group == 11), -1, a)
    a = jnp.where((group == 12) | (group == 13), CH, a)
    b = jnp.where((group == 10) | (group == 12), jnp.where(k == CW - 1, -1, far), b)
    b = jnp.where((group == 11) | (group == 13), jnp.where(k == 0, CW, far), b)
    return a, b


def kernel(
    lats, lons, fq_hbm, fkv_hbm, cq_hbm, ckv_hbm, out_hbm,
    fq, own, cq, cext, packed, sides, caps, cflat, atts, edges, table, table2, upkv,
    own_marks, side_marks, cap_marks, total, weight, largest, acc, outv,
    local, send, recv, osem,
):
    lat, lon = lax.axis_index("lat"), lax.axis_index("lon")
    up, down = lax.rem(lat + lats - 1, lats), lax.rem(lat + 1, lats)
    left, right = lax.rem(lon + lons - 1, lons), lax.rem(lon + 1, lons)

    loads = [
        pltpu.make_async_copy(fkv_hbm, own, local.at[0]),
        pltpu.make_async_copy(ckv_hbm, cext.at[CH : 2 * CH, CW : 2 * CW], local.at[1]),
        pltpu.make_async_copy(fq_hbm, fq, local.at[2]),
        pltpu.make_async_copy(cq_hbm, cq, local.at[3]),
    ]
    for load in loads:
        load.start()

    barrier = pltpu.get_barrier_semaphore()
    for other in (
        (up, lon), (down, lon), (lat, left), (lat, right),
        (up, left), (up, right), (down, left), (down, right),
    ):
        pl.semaphore_signal(barrier, inc=1, device_id=other, device_id_type=MESH)
    middle = lats // 2
    not_top, not_last = lat != 0, lat != lats - 1
    relay = (lat == 0) | (lat == lats - 1)
    linked = relay | (lat == middle - 1) | (lat == middle)
    across = lax.rem(lat + middle, lats)
    beside = jnp.where(lat < middle, middle - 1 - lat, lats + middle - 1 - lat)

    @pl.when(linked)
    def _():
        for other in (across, beside):
            pl.semaphore_signal(barrier, inc=1, device_id=(other, lon), device_id_type=MESH)

    def remote(number, source, target, device):
        return pltpu.make_async_remote_copy(
            src_ref=source, dst_ref=target, send_sem=send.at[number],
            recv_sem=recv.at[number], device_id=device, device_id_type=MESH,
        )

    mid = slice(CH, 2 * CH)
    west, centre, east = slice(0, CW), slice(CW, 2 * CW), slice(2 * CW, 3 * CW)
    coarse_lon = [
        remote(0, ckv_hbm, cext.at[mid, west], (lat, right)),
        remote(1, ckv_hbm, cext.at[mid, east], (lat, left)),
    ]
    coarse_lat = [
        remote(2, ckv_hbm, cext.at[0:CH, centre], (down, lon)),
        remote(3, ckv_hbm, cext.at[2 * CH : 3 * CH, centre], (up, lon)),
    ]
    coarse_corner = [
        remote(4 + 2 * n + m, cext.at[mid, side], cext.at[rows, side], device)
        for n, side in enumerate((west, east))
        for m, (rows, device) in enumerate(
            ((slice(0, CH), (down, lon)), (slice(2 * CH, 3 * CH), (up, lon)))
        )
    ]
    def strip_moves(number, low, high):
        source, target = slice(low, high), slice(PAD + low, PAD + high)
        return [
            remote(number, packed.at[1, source], sides.at[0, target], (lat, right)),
            remote(number + 1, packed.at[0, source], sides.at[1, target], (lat, left)),
        ]

    ends_lon = strip_moves(8, 0, CORNER) + strip_moves(25, EDGE - CORNER, EDGE)
    rest_lon = strip_moves(27, CORNER, EDGE - CORNER)
    via_top, via_last = lat == middle - 1, lat == middle

    def cap_move(number, arrival, source, slot, device):
        return pltpu.make_async_remote_copy(
            src_ref=source, dst_ref=caps.at[slot], send_sem=send.at[number],
            recv_sem=recv.at[arrival], device_id=(device, lon), device_id_type=MESH,
        )

    cap_down = cap_move(
        10, jnp.where(via_top, 24, 10), fkv_hbm.at[FH - RADIUS : FH],
        jnp.where(via_top, 2, 0), jnp.where(via_top, 0, down),
    )
    cap_up = cap_move(
        11, jnp.where(via_last, 24, 11), fkv_hbm.at[0:RADIUS],
        jnp.where(via_last, 2, 1), jnp.where(via_last, lats - 1, up),
    )
    cap_on = cap_move(
        24, jnp.where(lat == 0, 10, 11), caps.at[2],
        jnp.where(lat == 0, 0, 1), jnp.where(lat == 0, middle, middle - 1),
    )
    relayed = remote(24, fkv_hbm.at[0:RADIUS], caps.at[2], (lat, right))
    cap_from = [
        remote(10, fkv_hbm.at[0:RADIUS], caps.at[0], (lat, right)),
        remote(11, fkv_hbm.at[0:RADIUS], caps.at[1], (lat, right)),
    ]

    def when_down(action, *copies):
        @pl.when(not_last)
        def _():
            for copy in copies:
                getattr(copy, action)()

    def when_up(action, *copies):
        @pl.when(not_top)
        def _():
            for copy in copies:
                getattr(copy, action)()

    fine_corner = [
        remote(12 + 2 * n + m, sides.at[n, source], sides.at[n, target], device)
        for n in range(2)
        for m, (source, target, device) in enumerate(
            (
                (slice(PAD + EDGE - CORNER, PAD + EDGE), slice(PAD - CORNER, PAD), (down, lon)),
                (slice(PAD, PAD + CORNER), slice(PAD + EDGE, PAD + EDGE + CORNER), (up, lon)),
            )
        )
    ]
    base = CH * CW
    first_row, last_row = atts.at[0:CW], atts.at[base - CW : base]
    att_moves = [
        remote(16 + n, source, atts.at[base + 8 * n : base + 8 * n + 8], device)
        for n, (source, device) in enumerate(
            (
                (edges.at[8:16], (lat, right)),
                (edges.at[0:8], (lat, left)),
                (last_row, (down, lon)),
                (first_row, (up, lon)),
                (last_row, (down, right)),
                (last_row, (down, left)),
                (first_row, (up, right)),
                (first_row, (up, left)),
            )
        )
    ]

    pl.semaphore_wait(barrier, jnp.where(linked, 10, 8))

    for copy in coarse_lon:
        copy.start()
    when_down("start", coarse_lat[0], cap_down)
    when_up("start", coarse_lat[1], cap_up)

    loads[0].wait()
    cell, place = iota((EDGE, FH * 8), 0), iota((EDGE, FH * 8), 1)
    for n in range(2):
        wanted = cell // RADIUS * 8 + cell % RADIUS + 2 * n
        pick = jnp.where(place == wanted, 1.0, 0.0).astype(BF16)
        outer = own[:, n * (FW - 8) : n * (FW - 8) + 8, :]
        packed[n] = dot(pick, flat(outer)).astype(BF16)

    place = lax.rem(lat, middle)
    inner = (place >= 2) & (place < middle - 2)

    @pl.when(inner)
    def _():
        for copy in ends_lon:
            copy.start()

    for n in range(2):
        for low in (0, PAD + EDGE + CORNER):
            sides[n, low : low + PAD - CORNER] = jnp.zeros((PAD - CORNER, 2 * D), BF16)

    def clear(pole):
        gone = slice(2 * CH * pole, 2 * CH * pole + CH)
        cext[gone] = jnp.zeros((CH, 3 * CW, 2 * D), BF16)
        caps[pole] = jnp.zeros((RADIUS, FW, 2 * D), BF16)
        gone = slice(PAD + EDGE, PAD + EDGE + CORNER) if pole else slice(PAD - CORNER, PAD)
        for n in range(2):
            sides[n, gone] = jnp.zeros((CORNER, 2 * D), BF16)
        for group in (2, 4, 5) if not pole else (3, 6, 7):
            place = CH * CW + 8 * group
            atts[place : place + 8] = jnp.zeros((8, D), BF16)

    @pl.when(lat == 0)
    def _():
        clear(0)

    @pl.when(lat == lats - 1)
    def _():
        clear(1)

    pos = iota((CELLS, 1), 0)
    own_marks[0] = query_marks(pos // FW, pos % FW, CELLS)
    own_marks[1] = key_marks(pos // FW, pos % FW, CELLS, 0, FH)
    pos = iota((SIDE, 1), 0) + (6 * 10 - PAD)
    for n in range(2):
        side_marks[n] = key_marks(
            pos // 6 - 10, pos % 6 + (FW if n else -RADIUS), SIDE, lat * FH, lats * FH
        )
    pos = iota((CAP, 1), 0)
    for n in range(2):
        cap_marks[n] = key_marks(
            pos // FW + (FH if n else -RADIUS), pos % FW, CAP, lat * FH, lats * FH
        )
    lane = iota((1, CYCLE), 1)
    table[...] = spread(lane // (3 * CW) - 1, lane % (3 * CW) - CW, lat, lats)
    table2[...] = spread(*att_places(), lat, lats)

    first = iota((1, 128), 1) < 64

    def heads(query, scale):
        low = jnp.where(first, scale, 0.0).astype(BF16)
        high = jnp.where(first, 0.0, scale).astype(BF16)
        return query * low, query * high

    def lanes_of(pair, offset=0):
        return pl.ds(pair * 128 + offset, 128)

    def over_pairs(part):
        for pair in range(4):
            part(pair, 0)

    def own_part(pair, carry):
        lanes, vlanes = lanes_of(pair), lanes_of(pair, D)
        for block in range(3):
            rows = slice(8 * block, 8 * block + 8)
            low, high = max(8 * block - RADIUS, 0), min(8 * block + 8 + RADIUS, FH)
            count = (high - low) * FW
            query = fq[rows, :, lanes].reshape(8 * FW, 128)
            keys = jnp.concatenate(
                [own[low:high, :, lanes].reshape(count, 128), own_marks[1, low * FW : high * FW]],
                1,
            )
            values = jnp.concatenate(
                [own[low:high, :, vlanes].reshape(count, 128), jnp.ones((count, 128), BF16)], 1
            )
            marks = own_marks[0, 8 * block * FW : (8 * block + 8) * FW]
            found = attend(heads(query, 0.125), marks, keys, values)
            for ref, value in zip((total, weight, largest), found):
                ref[rows, :, lanes] = value.reshape(8, FW, 128)
        return carry

    loads[2].wait()
    for pair in (0, 1):
        own_part(pair, 0)
    for copy in coarse_lon:
        copy.wait_recv()
    when_down("start", *coarse_corner[0::2])
    when_up("start", *coarse_corner[1::2])

    @pl.when(relay)
    def _():
        relayed.wait_recv()
        cap_on.start()

    @pl.when(jnp.logical_not(inner))
    def _():
        for copy in ends_lon:
            copy.start()

    for copy in rest_lon:
        copy.start()

    for pair in (2, 3):
        own_part(pair, 0)
    when_up("wait_recv", coarse_lat[0], *coarse_corner[0::2])
    when_down("wait_recv", coarse_lat[1], *coarse_corner[1::2])
    loads[1].wait()
    loads[3].wait()

    cflat[...] = flat(cext[...])
    pos = iota((CH * CW, 1), 0)
    cq_marks = query_marks(pos // CW, pos % CW, CH * CW)
    pos = iota((CKEYS, 1), 0)
    ckey_marks = key_marks(
        pos // (3 * CW) - CH, pos % (3 * CW) - CW, CKEYS, lat * CH, lats * CH
    )
    for pair in range(4):
        lanes, vlanes = lanes_of(pair), lanes_of(pair, D)
        keys = jnp.concatenate([cflat[:, lanes], ckey_marks], 1)
        values = jnp.concatenate([cflat[:, vlanes], jnp.ones((CKEYS, 128), BF16)], 1)
        found = attend(
            heads(flat(cq[:, :, lanes]), 0.125), cq_marks, keys, values, stack=True
        )
        atts[0:base, lanes] = (found[0] / found[1]).astype(BF16)
    row, col = iota((16, base), 0), iota((16, base), 1)
    wanted = row % 8 * CW + jnp.where(row < 8, 0, CW - 1)
    pick = jnp.where((col == wanted) & (row % 8 < CH), 1.0, 0.0).astype(BF16)
    edges[...] = dot(pick, atts[0:base]).astype(BF16)
    att_lon = att_moves[0:2]
    att_down, att_up = att_moves[2:3] + att_moves[4:6], att_moves[3:4] + att_moves[6:8]
    for copy in att_lon:
        copy.start()
    when_down("start", *att_down)
    when_up("start", *att_up)

    start = (CH - 1) * 3 * CW
    for part in range(4):
        lanes = slice(part * 256, part * 256 + 256)
        upkv[:, lanes] = dot(table[...], cflat[start : start + CYCLE, lanes]).astype(BF16)

    def cross_part(pair, carry):
        lanes, vlanes = lanes_of(pair), lanes_of(pair, D)
        query = fq[:, :, lanes].reshape(CELLS, 128).astype(F32) * (0.125 * LOG2E)
        main = query.astype(BF16)
        rest = (query - main.astype(F32)).astype(BF16)
        heads_of = [
            jnp.concatenate([a, b], 1) for a, b in zip(heads(main, 1.0), heads(rest, 1.0))
        ]
        keys = jnp.concatenate([upkv[:, lanes], upkv[:, lanes]], 1)
        values = jnp.concatenate([upkv[:, vlanes], jnp.ones((CELLS, 128), BF16)], 1)
        found = attend(heads_of, None, keys, values, True)
        acc[:, :, lanes] = (found[0] / found[1]).reshape(FH, FW, 128)
        return carry

    for pair in (0, 1):
        cross_part(pair, 0)
    for copy in ends_lon:
        copy.wait_recv()
    when_down("start", *fine_corner[0::2])
    when_up("start", *fine_corner[1::2])
    for pair in (2, 3):
        cross_part(pair, 0)

    when_up("wait_recv", cap_from[0])
    when_down("wait_recv", cap_from[1])

    def halo_part(rows, cols, shape, marks, halo, halo_marks, count, pair):
        lanes, vlanes = lanes_of(pair), lanes_of(pair, D)
        query = flat(fq[rows, cols, lanes])
        keys = jnp.concatenate([halo[..., lanes].reshape(count, 128), halo_marks], 1)
        values = jnp.concatenate([halo[..., vlanes].reshape(count, 128), jnp.ones((count, 128), BF16)], 1)
        value, amount, top = attend(heads(query, 0.125), marks, keys, values, stack=True)
        old = largest[rows, cols, lanes].reshape(-1, 128)
        new = jnp.maximum(old, top)
        keep, add = jnp.exp(old - new), jnp.exp(top - new)
        largest[rows, cols, lanes] = new.reshape(shape)
        for ref, part in ((total, value), (weight, amount)):
            before = ref[rows, cols, lanes].reshape(-1, 128)
            ref[rows, cols, lanes] = (before * keep + part * add).reshape(shape)

    def cap_part(pair, carry):
        for n in range(2):
            low = n * (FH - RADIUS)
            marks = own_marks[0, low * FW : (low + RADIUS) * FW]
            halo_part(
                slice(low, low + RADIUS), slice(0, FW), (RADIUS, FW, 128), marks,
                caps.at[n], cap_marks[n], CAP, pair,
            )
        return carry

    over_pairs(cap_part)

    for copy in att_lon:
        copy.wait_recv()
    when_up("wait_recv", *att_down)
    when_down("wait_recv", *att_up)
    acc[...] += dot(table2[...], atts[...]).reshape(FH, FW, D)
    for copy in rest_lon:
        copy.wait_recv()
    when_up("wait_recv", *fine_corner[0::2])
    when_down("wait_recv", *fine_corner[1::2])

    pos = iota((FH * 8, 1), 0)
    outer_marks = [query_marks(pos // 8, pos % 8 + n * (FW - 8), FH * 8) for n in range(2)]

    def side_part(pair, carry):
        for n in range(2):
            low = n * (FW - 8)
            halo_part(
                slice(0, FH), slice(low, low + 8), (FH, 8, 128), outer_marks[n],
                sides.at[n], side_marks[n], SIDE, pair,
            )
        return carry

    over_pairs(side_part)

    fine = (total[...] / weight[...]).astype(BF16).astype(F32)
    outv[...] = (fine + acc[...]).astype(BF16)
    store = pltpu.make_async_copy(outv, out_hbm, osem)
    store.start()
    for copy in coarse_lon + ends_lon + rest_lon + att_lon:
        copy.wait_send()
    when_down(
        "wait_send", coarse_lat[0], cap_down, *coarse_corner[0::2], *fine_corner[0::2], *att_down
    )
    when_up(
        "wait_send", coarse_lat[1], cap_up, *coarse_corner[1::2], *fine_corner[1::2], *att_up
    )

    @pl.when(relay)
    def _():
        cap_on.wait_send()

    store.wait()


def shards(fine_query, fine_keyval, coarse_query, coarse_keyval, out_weight):
    lats, lons = lax.axis_size("lat"), lax.axis_size("lon")
    anywhere = pl.BlockSpec(memory_space=pl.ANY)
    dma, vmem = pltpu.SemaphoreType.DMA, pltpu.VMEM
    joined = pl.pallas_call(
        functools.partial(kernel, lats, lons),
        out_shape=jax.ShapeDtypeStruct(fine_query.shape, BF16),
        in_specs=[anywhere] * 4,
        out_specs=anywhere,
        scratch_shapes=[
            vmem((FH, FW, D), BF16),
            vmem((FH, FW, 2 * D), BF16),
            vmem((CH, CW, D), BF16),
            vmem((3 * CH, 3 * CW, 2 * D), BF16),
            vmem((2, EDGE, 2 * D), BF16),
            vmem((2, SIDE, 2 * D), BF16),
            vmem((3, RADIUS, FW, 2 * D), BF16),
            vmem((CKEYS, 2 * D), BF16),
            vmem((ATTS, D), BF16),
            vmem((16, D), BF16),
            vmem((CELLS, CYCLE), BF16),
            vmem((CELLS, ATTS), BF16),
            vmem((CELLS, 2 * D), BF16),
            vmem((2, CELLS, 128), BF16),
            vmem((2, SIDE, 128), BF16),
            vmem((2, CAP, 128), BF16),
            vmem((FH, FW, D), F32),
            vmem((FH, FW, D), F32),
            vmem((FH, FW, D), F32),
            vmem((FH, FW, D), F32),
            vmem((FH, FW, D), BF16),
            dma((4,)),
            dma((29,)),
            dma((29,)),
            dma,
        ],
        compiler_params=pltpu.CompilerParams(
            collective_id=0, has_side_effects=True, vmem_limit_bytes=56 << 20
        ),
        name="neighbourhood",
    )(fine_query, fine_keyval, coarse_query, coarse_keyval)
    return dot(joined, out_weight).astype(BF16)


def solution(mesh):
    tile = P("lat", "lon", None)
    return jax.shard_map(
        shards, mesh=mesh, in_specs=(tile, tile, tile, tile, P()), out_specs=tile,
        check_vma=False,
    )
```
